32 devices in a mesh: ep: 16 (over z, x, core), tp: 2 (over y).
Axes of the slice: x: 2, y: 2, z: 4, core: 2. Of those that a mesh axis runs over, the one named last changes fastest.
Arguments:
- attn: bfloat16 [2048, 2048], P('ep', 'tp'), may hold values from -6 to 6
- o_weight: bfloat16 [2048, 2048], P('tp'), may hold values from -0.125 to 0.125
- residual: bfloat16 [2048, 2048], P(('ep', 'tp')), may hold values from -6 to 6
- norm_gain: float32 [2048], replicated, may hold values from 0.5 to 2
- routes: int32 [2048, 6], P('ep'), may hold values from 0 to 15, all different within a row; in each aligned block of 64 rows (0 to 63, 64 to 127, ...) at most 32 rows name the same one
- route_logits: float32 [2048, 6], P('ep'), may hold values from -6 to 6
- expert_in: bfloat16 [16, 2, 2048, 1408], P('ep', None, None, 'tp'), may hold values from -0.125 to 0.125
- expert_out: bfloat16 [16, 2048, 1408], P('ep', None, 'tp'), may hold values from -0.15625 to 0.15625
- shared_in: bfloat16 [2, 2048, 1408], P(None, None, 'tp'), may hold values from -0.125 to 0.125
- shared_out: bfloat16 [2048, 1408], P(None, 'tp'), may hold values from -0.15625 to 0.15625
Outputs:
- block_out: bfloat16 [2048, 2048], P(('ep', 'tp'))
The draws below stay inside these ranges and needn't reach their ends.
Inputs may be any that keep to these rules, and one draw needn't show every extreme that they name: `routes`: each row names 6 different experts. Within each aligned block of 64 rows (the rows of one device) no expert is named by more than 32 rows, a bound that some block reaches.
All inputs are finite; a program needn't handle non-finite values.
Results may differ from the reference program's by a relative error of at most 0.0058.
Values may be sent and summed in bfloat16 or wider, within the bound.
A program may use at most 192 MiB of HBM per device.

```python
import math
import jax
import jax.numpy as jnp
import numpy as np
from jax import lax

D = 2048
HD = 2048
FF = 1408
SFF = 1408
TOP = 6
EXPERTS = 16
TOK_DEV = 64
TOKENS = 2048
CAP = 32


def level_of(key, shape, split, low, high):
    factor_of = 1.0
    for position, parts in split:
        steps = jax.random.uniform(jax.random.fold_in(jax.random.fold_in(key, 6), position), (parts,), jnp.float32, low / len(split), high / len(split))
        factor_of = factor_of * jnp.repeat(jnp.exp(steps), shape[position] // parts).reshape((-1,) + (1,) * (len(shape) - 1 - position))
    return factor_of


def routed_block(key, own, number, rows, number_of, top, bound, skew):
    sequence = jax.random.permutation(key, number_of)
    heavy_load, ordinary = portions_of(number_of, rows * top, bound, skew, True), portions_of(number_of, rows * top, bound, skew, False)
    places = jnp.arange(number_of)

    def named(sizes, offset_by):
        used = int((sizes > 0).sum())
        fixed = max(1, used // 4)
        moved = fixed + (places - fixed + offset_by * (used - fixed)) % max(1, number_of - fixed)
        return jnp.zeros((number_of,), jnp.int32).at[sequence[jnp.where(places < fixed, places, moved)]].set(jnp.asarray(sizes, jnp.int32))

    sizes = jnp.where(number % 4 == 0, named(heavy_load, number // 4), named(ordinary, number - number // 4 - 1))
    mixed = jax.random.permutation(jax.random.fold_in(own, 3), number_of)
    donor, receiver = mixed[0:number_of // 2 * 2:2], mixed[1:number_of // 2 * 2:2]
    room = jnp.minimum(sizes[donor] - 1, bound - sizes[receiver]) // 2
    room = jnp.where((donor == sequence[0]) | (receiver == sequence[0]) | (sizes[receiver] == 0), 0, jnp.maximum(room, 0))
    moved = jax.random.randint(jax.random.fold_in(own, 4), (number_of // 2,), 0, 1 << 20) % (room + 1)
    sizes = sizes.at[donor].add(-moved).at[receiver].add(moved)
    members = jnp.searchsorted(jnp.cumsum(sizes), jnp.arange(rows * top), side="right").astype(jnp.int32)
    listing = members.reshape(top, rows).T
    listing = listing[jax.random.permutation(jax.random.fold_in(own, 1), rows)]
    offset_by = jax.random.randint(jax.random.fold_in(own, 2), (rows, 1), 0, top)
    return jnp.take_along_axis(listing, (jnp.arange(top)[None, :] + offset_by) % top, axis=1)


def portions_of(amount, total, most, slope, full):
    loads = [(1 << 20) // math.isqrt(rank ** slope) + 1 for rank in range(1, amount + 1)]
    largest = most if full else min(most, max(-(-total // amount), total * loads[0] // sum(loads)))
    least = 1 if total - largest >= amount - 1 else 0
    holding, spare = [largest] + [least] * (amount - 1), total - largest - least * (amount - 1)
    while spare > 0:
        candidates = [i for i in range(1, amount) if holding[i] < largest] or [i for i in range(1, amount) if holding[i] < most]
        pool, remaining = sum([loads[i] for i in candidates]), spare
        for i in candidates:
            addition = min(most - holding[i], max(1, remaining * loads[i] // pool), spare)
            holding[i] = holding[i] + addition
            spare = spare - addition
    return np.array(holding)


def scatter_about(rng, dims, scale, reach, shards=(), kind=jnp.bfloat16):
    result = scale * jax.random.normal(rng, dims, jnp.float32)
    if shards:
        result = result * level_of(rng, dims, shards, -0.22, 0.18)
    return jnp.clip(result, -reach, reach).astype(kind)


def setup_inputs(seed: int = 0) -> dict:
    keys = jax.random.split(jax.random.key(seed), 11)
    attn = scatter_about(keys[0], (TOKENS, HD), 1.0, 6.0, ((0, 16), (1, 2)))
    o_weight = scatter_about(keys[1], (HD, D), HD ** -0.5, 0.125, ((0, 2),))
    residual = scatter_about(keys[2], (TOKENS, D), 1.0, 6.0, ((0, 32),))
    norm_gain = jnp.clip(jax.random.uniform(keys[3], (D,), jnp.float32, 0.5, 2.0), 0.5, 2.0)
    routes_keys = jax.random.split(jax.random.fold_in(keys[4], 1), TOKENS // TOK_DEV)
    routes_turns = jax.random.permutation(jax.random.fold_in(keys[4], 3), TOKENS // TOK_DEV)
    routes = jax.vmap(lambda own, number: routed_block(jax.random.fold_in(keys[4], 2), own, number, TOK_DEV, EXPERTS, TOP, CAP, 2))(routes_keys, routes_turns).reshape((TOKENS, TOP))
    route_logits = scatter_about(keys[5], (TOKENS, TOP), 1.5, 6.0, ((0, 16),), jnp.float32)
    expert_in = scatter_about(keys[6], (EXPERTS, 2, D, FF), D ** -0.5, 0.125, ((0, 16), (3, 2)))
    expert_out = scatter_about(keys[7], (EXPERTS, D, FF), FF ** -0.5, 0.15625, ((0, 16), (2, 2)))
    shared_in = scatter_about(keys[8], (2, D, SFF), D ** -0.5, 0.125, ((2, 2),))
    shared_out = scatter_about(keys[9], (D, SFF), SFF ** -0.5, 0.15625, ((1, 2),))
    return dict(attn=attn, o_weight=o_weight, residual=residual, norm_gain=norm_gain, routes=routes, route_logits=route_logits, expert_in=expert_in, expert_out=expert_out, shared_in=shared_in, shared_out=shared_out)


def reference(attn, o_weight, residual, norm_gain, routes, route_logits, expert_in, expert_out, shared_in, shared_out):
    hidden = residual.astype(jnp.float32) + jnp.dot(attn, o_weight, preferred_element_type=jnp.float32)
    inv_norm = lax.rsqrt(lax.optimization_barrier(jnp.mean(hidden * hidden, axis=-1, keepdims=True)) + 1e-06)
    normed = (hidden * inv_norm * norm_gain).astype(jnp.bfloat16)
    sigmoids = jax.nn.sigmoid(route_logits)
    route_weight = 2.446 * sigmoids / lax.optimization_barrier(jnp.sum(sigmoids, axis=-1, keepdims=True))
    blocks = TOKENS // TOK_DEV
    flat_routes = routes.reshape(blocks, TOK_DEV * TOP)
    onehot = (flat_routes[:, :, None] == jnp.arange(EXPERTS, dtype=jnp.int32)[None, None, :]).astype(jnp.int32)
    ranks = lax.optimization_barrier(jnp.sum((jnp.cumsum(onehot, axis=1) - onehot) * onehot, axis=2))
    depth = blocks * CAP
    places = flat_routes * depth + jnp.arange(blocks, dtype=jnp.int32)[:, None] * CAP + ranks
    token_ids = jnp.repeat(jnp.arange(TOKENS, dtype=jnp.int32), TOP)
    slot_tokens = jnp.full((EXPERTS * depth,), TOKENS, jnp.int32).at[places.reshape(-1)].set(token_ids)
    slot_weights = jnp.zeros((EXPERTS * depth,), jnp.float32).at[places.reshape(-1)].set(route_weight.reshape(-1))
    padded = jnp.concatenate([normed, jnp.zeros((1, D), jnp.bfloat16)], axis=0)

    def one_expert(accumulated, item):
        token_index, slot_scale, w_in, w_out = item
        chosen = padded[token_index]
        gate_val = jnp.dot(chosen, w_in[0], preferred_element_type=jnp.float32)
        up_val = jnp.dot(chosen, w_in[1], preferred_element_type=jnp.float32)
        active = (jax.nn.silu(gate_val) * up_val).astype(jnp.bfloat16)
        values = jnp.dot(active, w_out.T, preferred_element_type=jnp.float32)
        return (accumulated.at[token_index].add(slot_scale[:, None] * values), None)
    start_total = jnp.zeros((TOKENS + 1, D), jnp.float32)
    accumulated, unused = lax.scan(one_expert, start_total, (slot_tokens.reshape(EXPERTS, depth), slot_weights.reshape(EXPERTS, depth), expert_in, expert_out))
    shared_gate = jnp.dot(normed, shared_in[0], preferred_element_type=jnp.float32)
    shared_up = jnp.dot(normed, shared_in[1], preferred_element_type=jnp.float32)
    shared_act = (jax.nn.silu(shared_gate) * shared_up).astype(jnp.bfloat16)
    shared_val = jnp.dot(shared_act, shared_out.T, preferred_element_type=jnp.float32)
    return (hidden + accumulated[:TOKENS] + shared_val).astype(jnp.bfloat16)
```

```python
import jax
import jax.numpy as jnp
from jax import lax
from jax.sharding import PartitionSpec as P


def slot_places(route_rows, capacity, experts):
    flat_routes = route_rows.reshape(-1)
    onehot = (flat_routes[:, None] == jnp.arange(experts, dtype=jnp.int32)[None, :]).astype(
        jnp.int32
    )
    before = jnp.cumsum(onehot, axis=0) - onehot
    ranks = jnp.sum(before * onehot, axis=1)
    return flat_routes * capacity + ranks


def fill_slots(source_rows, places, capacity, experts, topk):
    copies = jnp.repeat(source_rows, topk, axis=0)
    empty_slots = jnp.zeros((experts * capacity, source_rows.shape[1]), source_rows.dtype)
    return empty_slots.at[places].set(copies)


def route_weights(logits):
    sigmoids = jax.nn.sigmoid(logits)
    return 2.446 * sigmoids / jnp.sum(sigmoids, axis=-1, keepdims=True)


def expert_part(slots, w_in, w_out):
    gate_val = jnp.einsum("slcd,ldf->slcf", slots, w_in[:, 0], preferred_element_type=jnp.float32)
    up_val = jnp.einsum("slcd,ldf->slcf", slots, w_in[:, 1], preferred_element_type=jnp.float32)
    active = (jax.nn.silu(gate_val) * up_val).astype(jnp.bfloat16)
    return jnp.einsum("slcf,ldf->slcd", active, w_out, preferred_element_type=jnp.float32)


def shared_part(source_rows, s_in, s_out):
    gate_val = jnp.dot(source_rows, s_in[0], preferred_element_type=jnp.float32)
    up_val = jnp.dot(source_rows, s_in[1], preferred_element_type=jnp.float32)
    active = (jax.nn.silu(gate_val) * up_val).astype(jnp.bfloat16)
    return jnp.einsum("tf,df->td", active, s_out, preferred_element_type=jnp.float32)


def combine_slots(values, places, weights, topk):
    picked = values[places].reshape(-1, topk, values.shape[1])
    return jnp.sum(picked * weights[:, :, None], axis=1)


def slotted_shards(
    attn,
    o_weight,
    residual,
    norm_gain,
    routes,
    route_logits,
    expert_in,
    expert_out,
    shared_in,
    shared_out,
):
    tok_rows = residual.shape[0]
    width = residual.shape[1]
    topk = routes.shape[1]
    tp_count = lax.axis_size("tp")
    ep_count = lax.axis_size("ep")
    local_experts = expert_in.shape[0]
    experts = local_experts * ep_count
    capacity = max(2, (4 * tok_rows * topk + 3 * experts - 1) // (3 * experts))
    attn_out = lax.psum_scatter(
        jnp.dot(attn, o_weight, preferred_element_type=jnp.float32),
        "tp",
        scatter_dimension=0,
        tiled=True,
    )
    hidden = residual.astype(jnp.float32) + attn_out
    inv_norm = lax.rsqrt(jnp.mean(hidden * hidden, axis=-1, keepdims=True) + 1e-06)
    normed = (hidden * inv_norm * norm_gain).astype(jnp.bfloat16)
    group_rows = lax.all_gather(normed, "tp", axis=0, tiled=True)
    group_cap = tp_count * capacity
    places = slot_places(routes, group_cap, experts)
    outgoing = fill_slots(group_rows, places, group_cap, experts, topk)
    incoming = lax.all_to_all(outgoing, "ep", split_axis=0, concat_axis=0, tiled=True)
    partial_value = expert_part(
        incoming.reshape(ep_count, local_experts, group_cap, width), expert_in, expert_out
    )
    returned = lax.all_to_all(
        partial_value.reshape(-1, width), "ep", split_axis=0, concat_axis=0, tiled=True
    )
    mixture = combine_slots(returned, places, route_weights(route_logits), topk)
    mixture = mixture + shared_part(group_rows, shared_in, shared_out)
    moe_sum = lax.psum_scatter(mixture, "tp", scatter_dimension=0, tiled=True)
    return (hidden + moe_sum).astype(jnp.bfloat16)


def tp_sum_scatter(rows):
    count = lax.axis_size("tp")
    if count != 2:
        return lax.psum_scatter(rows, "tp", scatter_dimension=0, tiled=True)
    me = lax.axis_index("tp")
    each = rows.shape[0] // count
    away = lax.dynamic_slice_in_dim(rows, (1 - me) * each, each, 0).astype(jnp.bfloat16)
    arrived = lax.ppermute(away, "tp", [(0, 1), (1, 0)])
    own = lax.dynamic_slice_in_dim(rows, me * each, each, 0)
    return own + arrived.astype(jnp.float32)


def dense_shards(
    attn,
    o_weight,
    residual,
    norm_gain,
    routes,
    route_logits,
    expert_in,
    expert_out,
    shared_in,
    shared_out,
):
    local_experts = expert_in.shape[0]
    ep_count = lax.axis_size("ep")
    experts = local_experts * ep_count
    ep_me = lax.axis_index("ep")
    weights = route_weights(route_logits)
    chosen = routes[:, :, None] == jnp.arange(experts, dtype=jnp.int32)[None, None, :]
    dense_weights = jnp.sum(jnp.where(chosen, weights[:, :, None], 0.0), axis=1)
    all_weights = lax.all_gather(dense_weights, "ep", axis=0, tiled=True)
    my_weights = lax.dynamic_slice_in_dim(all_weights, ep_me * local_experts, local_experts, 1)

    attn_out = tp_sum_scatter(jnp.dot(attn, o_weight, preferred_element_type=jnp.float32))
    hidden = residual.astype(jnp.float32) + attn_out
    inv_norm = lax.rsqrt(jnp.mean(hidden * hidden, axis=-1, keepdims=True) + 1e-06)
    normed = (hidden * inv_norm * norm_gain).astype(jnp.bfloat16)
    all_rows = lax.all_gather(normed, ("ep", "tp"), axis=0, tiled=True)
    group_rows = lax.all_gather(normed, "tp", axis=0, tiled=True) if lax.axis_size("tp") != 2 else None
    if group_rows is None:
        other = lax.ppermute(normed, "tp", [(0, 1), (1, 0)])
        first = lax.axis_index("tp") == 0
        group_rows = jnp.concatenate(
            [jnp.where(first, normed, other), jnp.where(first, other, normed)], axis=0
        )
    shared = tp_sum_scatter(shared_part(group_rows, shared_in, shared_out))
    partial = None
    for item in range(local_experts):
        gate_val = jnp.dot(all_rows, expert_in[item, 0], preferred_element_type=jnp.float32)
        up_val = jnp.dot(all_rows, expert_in[item, 1], preferred_element_type=jnp.float32)
        active = (jax.nn.silu(gate_val) * up_val).astype(jnp.bfloat16)
        value = jnp.einsum("tf,df->td", active, expert_out[item], preferred_element_type=jnp.float32)
        value = value * my_weights[:, item : item + 1]
        partial = value if partial is None else partial + value
    mixture = lax.psum_scatter(
        partial.astype(jnp.bfloat16), ("ep", "tp"), scatter_dimension=0, tiled=True
    )
    return (hidden + shared + mixture.astype(jnp.float32)).astype(jnp.bfloat16)


def shards(*args):
    routes, expert_in = args[4], args[6]
    experts = expert_in.shape[0] * lax.axis_size("ep")
    if experts <= 4 * routes.shape[1]:
        return dense_shards(*args)
    return slotted_shards(*args)


def solution(mesh):
    in_specs = (
        P("ep", "tp"),
        P("tp", None),
        P(("ep", "tp"), None),
        P(),
        P("ep", None),
        P("ep", None),
        P("ep", None, None, "tp"),
        P("ep", None, "tp"),
        P(None, None, "tp"),
        P(None, "tp"),
    )
    out_specs = P(("ep", "tp"), None)
    return jax.shard_map(shards, mesh=mesh, in_specs=in_specs, out_specs=out_specs, check_vma=False)
```

```python
import jax
import jax.numpy as jnp
from jax import lax
from jax.experimental import pallas as pl
from jax.experimental.pallas import tpu as pltpu
from jax.sharding import PartitionSpec as P

PIECES = 4


def slot_places(route_rows, capacity, experts):
    flat_routes = route_rows.reshape(-1)
    onehot = (flat_routes[:, None] == jnp.arange(experts, dtype=jnp.int32)[None, :]).astype(
        jnp.int32
    )
    before = jnp.cumsum(onehot, axis=0) - onehot
    ranks = jnp.sum(before * onehot, axis=1)
    return flat_routes * capacity + ranks


def fill_slots(source_rows, places, capacity, experts, topk):
    copies = jnp.repeat(source_rows, topk, axis=0)
    empty_slots = jnp.zeros((experts * capacity, source_rows.shape[1]), source_rows.dtype)
    return empty_slots.at[places].set(copies)


def route_weights(logits):
    sigmoids = jax.nn.sigmoid(logits)
    return 2.446 * sigmoids / jnp.sum(sigmoids, axis=-1, keepdims=True)


def expert_part(slots, w_in, w_out):
    gate_val = jnp.einsum("slcd,ldf->slcf", slots, w_in[:, 0], preferred_element_type=jnp.float32)
    up_val = jnp.einsum("slcd,ldf->slcf", slots, w_in[:, 1], preferred_element_type=jnp.float32)
    active = (jax.nn.silu(gate_val) * up_val).astype(jnp.bfloat16)
    return jnp.einsum("slcf,ldf->slcd", active, w_out, preferred_element_type=jnp.float32)


def shared_part(source_rows, s_in, s_out):
    gate_val = jnp.dot(source_rows, s_in[0], preferred_element_type=jnp.float32)
    up_val = jnp.dot(source_rows, s_in[1], preferred_element_type=jnp.float32)
    active = (jax.nn.silu(gate_val) * up_val).astype(jnp.bfloat16)
    return jnp.einsum("tf,df->td", active, s_out, preferred_element_type=jnp.float32)


def combine_slots(values, places, weights, topk):
    picked = values[places].reshape(-1, topk, values.shape[1])
    return jnp.sum(picked * weights[:, :, None], axis=1)


def slotted_shards(
    attn,
    o_weight,
    residual,
    norm_gain,
    routes,
    route_logits,
    expert_in,
    expert_out,
    shared_in,
    shared_out,
):
    tok_rows = residual.shape[0]
    width = residual.shape[1]
    topk = routes.shape[1]
    tp_count = lax.axis_size("tp")
    ep_count = lax.axis_size("ep")
    local_experts = expert_in.shape[0]
    experts = local_experts * ep_count
    capacity = max(2, (4 * tok_rows * topk + 3 * experts - 1) // (3 * experts))
    attn_out = lax.psum_scatter(
        jnp.dot(attn, o_weight, preferred_element_type=jnp.float32),
        "tp",
        scatter_dimension=0,
        tiled=True,
    )
    hidden = residual.astype(jnp.float32) + attn_out
    inv_norm = lax.rsqrt(jnp.mean(hidden * hidden, axis=-1, keepdims=True) + 1e-06)
    normed = (hidden * inv_norm * norm_gain).astype(jnp.bfloat16)
    group_rows = lax.all_gather(normed, "tp", axis=0, tiled=True)
    group_cap = tp_count * capacity
    places = slot_places(routes, group_cap, experts)
    outgoing = fill_slots(group_rows, places, group_cap, experts, topk)
    incoming = lax.all_to_all(outgoing, "ep", split_axis=0, concat_axis=0, tiled=True)
    partial_value = expert_part(
        incoming.reshape(ep_count, local_experts, group_cap, width), expert_in, expert_out
    )
    returned = lax.all_to_all(
        partial_value.reshape(-1, width), "ep", split_axis=0, concat_axis=0, tiled=True
    )
    mixture = combine_slots(returned, places, route_weights(route_logits), topk)
    mixture = mixture + shared_part(group_rows, shared_in, shared_out)
    moe_sum = lax.psum_scatter(mixture, "tp", scatter_dimension=0, tiled=True)
    return (hidden + moe_sum).astype(jnp.bfloat16)


def place():
    ep = lax.axis_index("ep")
    return lax.div(ep, 4), lax.rem(lax.div(ep, 2), 2), lax.rem(ep, 2), lax.axis_index("tp")


def device_at(z, x, core, y):
    return (z * 4 + x * 2 + core, y)


def peers(z, x, core, y):
    along_z = [device_at(lax.rem(z + step, 4), x, core, y) for step in (1, 2, 3)]
    return (
        along_z,
        device_at(z, 1 - x, core, y),
        device_at(z, x, 1 - core, y),
        device_at(z, x, core, 1 - y),
    )


def greet(along_z, x_peer, core_peer, y_peer):
    barrier = pltpu.get_barrier_semaphore()
    for peer in (*along_z, x_peer, core_peer, y_peer):
        pl.semaphore_signal(
            barrier, inc=1, device_id=peer, device_id_type=pl.DeviceIdType.MESH
        )
    pl.semaphore_wait(barrier, 6)


def remote(src, dst, send_sem, recv_sem, peer):
    copy = pltpu.make_async_remote_copy(
        src_ref=src,
        dst_ref=dst,
        send_sem=send_sem,
        recv_sem=recv_sem,
        device_id=peer,
        device_id_type=pl.DeviceIdType.MESH,
    )
    copy.start()
    return copy


def gather_kernel(in_ref, out_ref, own_sem, z_send, z_recv, send, recv):
    z, x, core, y = place()
    along_z, x_peer, core_peer, y_peer = peers(z, x, core, y)
    rows = in_ref.shape[0] // PIECES
    own = pltpu.make_async_copy(in_ref, out_ref.at[z, x, core, y], own_sem)
    own.start()
    greet(along_z, x_peer, core_peer, y_peer)
    started = []
    z_copies = []
    for q in range(PIECES):
        piece = pl.ds(q * rows, rows)
        z_copies.append(
            [
                remote(
                    in_ref.at[piece],
                    out_ref.at[z, x, core, y, piece],
                    z_send.at[q, i],
                    z_recv.at[q, i],
                    along_z[i],
                )
                for i in range(3)
            ]
        )
    own.wait()
    waiting = []
    for q in range(PIECES):
        for copy in z_copies[q]:
            copy.wait_recv()
        part = out_ref.at[:, x, core, y, pl.ds(q * rows, rows)]
        peer = x_peer if q % 2 == 0 else y_peer
        waiting.append(remote(part, part, send.at[q, 0], recv.at[q, 0], peer))
    for q in range(PIECES):
        waiting[q].wait_recv()
        started.append(waiting[q])
        piece = pl.ds(q * rows, rows)
        if q % 2 == 0:
            part, peer = out_ref.at[:, :, core, y, piece], y_peer
        else:
            part, peer = out_ref.at[:, x, core, :, piece], x_peer
        waiting[q] = remote(part, part, send.at[q, 1], recv.at[q, 1], peer)
    for q in range(PIECES):
        waiting[q].wait_recv()
        started.append(waiting[q])
        part = out_ref.at[:, :, core, :, pl.ds(q * rows, rows)]
        waiting[q] = remote(part, part, send.at[q, 2], recv.at[q, 2], core_peer)
    for q in range(PIECES):
        waiting[q].wait_recv()
        started.append(waiting[q])
    for copies in z_copies:
        started.extend(copies)
    for copy in started:
        copy.wait_send()


def gather_rows(normed):
    rows, width = normed.shape
    out = pl.pallas_call(
        gather_kernel,
        out_shape=jax.ShapeDtypeStruct((4, 2, 2, 2, rows, width), normed.dtype),
        in_specs=[pl.BlockSpec(memory_space=pltpu.VMEM)],
        out_specs=pl.BlockSpec(memory_space=pl.ANY),
        scratch_shapes=[
            pltpu.SemaphoreType.DMA,
            pltpu.SemaphoreType.DMA((PIECES, 3)),
            pltpu.SemaphoreType.DMA((PIECES, 3)),
            pltpu.SemaphoreType.DMA((PIECES, 3)),
            pltpu.SemaphoreType.DMA((PIECES, 3)),
        ],
        compiler_params=pltpu.CompilerParams(collective_id=0, has_side_effects=True),
    )(normed)
    return out.reshape(-1, width)


def scatter_kernel(
    in_ref, out_ref, in0, in1, in2, in3, sum1, sum2, sum3, z_send, z_recv, send, recv
):
    z, x, core, y = place()
    along_z, x_peer, core_peer, y_peer = peers(z, x, core, y)
    rows = in_ref.shape[4] // PIECES
    f32 = jnp.float32
    greet(along_z, x_peer, core_peer, y_peer)
    started = []
    waiting = []
    for q in range(PIECES):
        part = in_ref.at[:, :, 1 - core, :, pl.ds(q * rows, rows)]
        waiting.append(remote(part, in0.at[q], send.at[q, 0], recv.at[q, 0], core_peer))
    for q in range(PIECES):
        waiting[q].wait_recv()
        started.append(waiting[q])
        piece = pl.ds(q * rows, rows)

        def add_core(i, carry):
            a, b, c = lax.div(i, 4), lax.rem(lax.div(i, 2), 2), lax.rem(i, 2)
            total = in_ref[a, b, core, c, piece].astype(f32) + in0[q, a, b, c].astype(f32)
            sum1[q, a, b, c] = total.astype(sum1.dtype)
            return carry

        lax.fori_loop(0, 16, add_core, 0)
        if q % 2 == 0:
            part, peer = sum1.at[q, :, 1 - x], x_peer
        else:
            part, peer = sum1.at[q, :, :, 1 - y], y_peer
        waiting[q] = remote(part, in1.at[q], send.at[q, 1], recv.at[q, 1], peer)
    for q in range(PIECES):
        waiting[q].wait_recv()
        started.append(waiting[q])

        def add_first(i, carry):
            a, b = lax.div(i, 2), lax.rem(i, 2)
            mine = sum1[q, a, x, b] if q % 2 == 0 else sum1[q, a, b, y]
            sum2[q, a, b] = (mine.astype(f32) + in1[q, a, b].astype(f32)).astype(sum2.dtype)
            return carry

        lax.fori_loop(0, 8, add_first, 0)
        if q % 2 == 0:
            part, peer = sum2.at[q, :, 1 - y], y_peer
        else:
            part, peer = sum2.at[q, :, 1 - x], x_peer
        waiting[q] = remote(part, in2.at[q], send.at[q, 2], recv.at[q, 2], peer)
    z_copies = []
    for q in range(PIECES):
        waiting[q].wait_recv()
        started.append(waiting[q])
        keep = y if q % 2 == 0 else x

        def add_second(a, carry):
            total = sum2[q, a, keep].astype(f32) + in2[q, a].astype(f32)
            sum3[q, a] = total.astype(sum3.dtype)
            return carry

        lax.fori_loop(0, 4, add_second, 0)
        z_copies.append(
            [
                remote(
                    sum3.at[q, lax.rem(z + i + 1, 4)],
                    in3.at[q, i],
                    z_send.at[q, i],
                    z_recv.at[q, i],
                    along_z[i],
                )
                for i in range(3)
            ]
        )
    for q in range(PIECES):
        for copy in z_copies[q]:
            copy.wait_recv()
            started.append(copy)
        total = sum3[q, z].astype(f32) + in3[q, 0].astype(f32)
        total = total + (in3[q, 1].astype(f32) + in3[q, 2].astype(f32))
        out_ref[pl.ds(q * rows, rows)] = total
    for copy in started:
        copy.wait_send()


def scatter_sum(partial):
    rows, width = partial.shape[0] // 32, partial.shape[1]
    piece = (rows // PIECES, width)
    kind = partial.dtype
    return pl.pallas_call(
        scatter_kernel,
        out_shape=jax.ShapeDtypeStruct((rows, width), jnp.float32),
        in_specs=[pl.BlockSpec(memory_space=pltpu.VMEM)],
        out_specs=pl.BlockSpec(memory_space=pltpu.VMEM),
        scratch_shapes=[
            pltpu.VMEM((PIECES, 4, 2, 2, *piece), kind),
            pltpu.VMEM((PIECES, 4, 2, *piece), kind),
            pltpu.VMEM((PIECES, 4, *piece), kind),
            pltpu.VMEM((PIECES, 3, *piece), kind),
            pltpu.VMEM((PIECES, 4, 2, 2, *piece), kind),
            pltpu.VMEM((PIECES, 4, 2, *piece), kind),
            pltpu.VMEM((PIECES, 4, *piece), kind),
            pltpu.SemaphoreType.DMA((PIECES, 3)),
            pltpu.SemaphoreType.DMA((PIECES, 3)),
            pltpu.SemaphoreType.DMA((PIECES, 3)),
            pltpu.SemaphoreType.DMA((PIECES, 3)),
        ],
        compiler_params=pltpu.CompilerParams(
            collective_id=1, has_side_effects=True, vmem_limit_bytes=60 * 1024 * 1024
        ),
    )(partial.reshape(4, 2, 2, 2, rows, width))


def tp_sum_scatter(rows):
    count = lax.axis_size("tp")
    if count != 2:
        return lax.psum_scatter(rows, "tp", scatter_dimension=0, tiled=True)
    me = lax.axis_index("tp")
    each = rows.shape[0] // count
    away = lax.dynamic_slice_in_dim(rows, (1 - me) * each, each, 0).astype(jnp.bfloat16)
    arrived = lax.ppermute(away, "tp", [(0, 1), (1, 0)])
    own = lax.dynamic_slice_in_dim(rows, me * each, each, 0)
    return own + arrived.astype(jnp.float32)


def dense_shards(
    attn,
    o_weight,
    residual,
    norm_gain,
    routes,
    route_logits,
    expert_in,
    expert_out,
    shared_in,
    shared_out,
):
    local_experts = expert_in.shape[0]
    ep_count = lax.axis_size("ep")
    experts = local_experts * ep_count
    ep_me = lax.axis_index("ep")
    weights = route_weights(route_logits)
    chosen = routes[:, :, None] == jnp.arange(experts, dtype=jnp.int32)[None, None, :]
    dense_weights = jnp.sum(jnp.where(chosen, weights[:, :, None], 0.0), axis=1)
    all_weights = lax.all_gather(dense_weights, "ep", axis=0, tiled=True)
    my_weights = lax.dynamic_slice_in_dim(all_weights, ep_me * local_experts, local_experts, 1)

    attn_out = tp_sum_scatter(jnp.dot(attn, o_weight, preferred_element_type=jnp.float32))
    hidden = residual.astype(jnp.float32) + attn_out
    inv_norm = lax.rsqrt(jnp.mean(hidden * hidden, axis=-1, keepdims=True) + 1e-06)
    normed = (hidden * inv_norm * norm_gain).astype(jnp.bfloat16)
    all_rows = gather_rows(normed)
    group = routes.shape[0]
    group_rows = lax.dynamic_slice_in_dim(all_rows, ep_me * group, group, 0)
    shared = shared_part(group_rows, shared_in, shared_out)
    partial = None
    for item in range(local_experts):
        gate_val = jnp.dot(all_rows, expert_in[item, 0], preferred_element_type=jnp.float32)
        up_val = jnp.dot(all_rows, expert_in[item, 1], preferred_element_type=jnp.float32)
        active = (jax.nn.silu(gate_val) * up_val).astype(jnp.bfloat16)
        value = jnp.einsum("tf,df->td", active, expert_out[item], preferred_element_type=jnp.float32)
        value = value * my_weights[:, item : item + 1]
        partial = value if partial is None else partial + value
    partial = partial.astype(jnp.bfloat16)
    own = lax.dynamic_slice_in_dim(partial, ep_me * group, group, 0).astype(jnp.float32) + shared
    partial = lax.dynamic_update_slice_in_dim(
        partial, own.astype(jnp.bfloat16), ep_me * group, 0
    )
    return (hidden + scatter_sum(partial)).astype(jnp.bfloat16)


def shards(*args):
    routes, expert_in = args[4], args[6]
    experts = expert_in.shape[0] * lax.axis_size("ep")
    spans = lax.axis_size("ep") == 16 and lax.axis_size("tp") == 2
    if spans and experts <= 4 * routes.shape[1]:
        return dense_shards(*args)
    return slotted_shards(*args)


def solution(mesh):
    in_specs = (
        P("ep", "tp"),
        P("tp", None),
        P(("ep", "tp"), None),
        P(),
        P("ep", None),
        P("ep", None),
        P("ep", None, None, "tp"),
        P("ep", None, "tp"),
        P(None, None, "tp"),
        P(None, "tp"),
    )
    out_specs = P(("ep", "tp"), None)
    return jax.shard_map(shards, mesh=mesh, in_specs=in_specs, out_specs=out_specs, check_vma=False)
```

```python
import jax
import jax.numpy as jnp
from jax import lax
from jax.experimental import pallas as pl
from jax.experimental.pallas import tpu as pltpu
from jax.sharding import PartitionSpec as P

PIECES = 4


def slot_places(route_rows, capacity, experts):
    flat_routes = route_rows.reshape(-1)
    onehot = (flat_routes[:, None] == jnp.arange(experts, dtype=jnp.int32)[None, :]).astype(
        jnp.int32
    )
    before = jnp.cumsum(onehot, axis=0) - onehot
    ranks = jnp.sum(before * onehot, axis=1)
    return flat_routes * capacity + ranks


def fill_slots(source_rows, places, capacity, experts, topk):
    copies = jnp.repeat(source_rows, topk, axis=0)
    empty_slots = jnp.zeros((experts * capacity, source_rows.shape[1]), source_rows.dtype)
    return empty_slots.at[places].set(copies)


def route_weights(logits):
    sigmoids = jax.nn.sigmoid(logits)
    return 2.446 * sigmoids / jnp.sum(sigmoids, axis=-1, keepdims=True)


def expert_part(slots, w_in, w_out):
    gate_val = jnp.einsum("slcd,ldf->slcf", slots, w_in[:, 0], preferred_element_type=jnp.float32)
    up_val = jnp.einsum("slcd,ldf->slcf", slots, w_in[:, 1], preferred_element_type=jnp.float32)
    active = (jax.nn.silu(gate_val) * up_val).astype(jnp.bfloat16)
    return jnp.einsum("slcf,ldf->slcd", active, w_out, preferred_element_type=jnp.float32)


def shared_part(source_rows, s_in, s_out):
    gate_val = jnp.dot(source_rows, s_in[0], preferred_element_type=jnp.float32)
    up_val = jnp.dot(source_rows, s_in[1], preferred_element_type=jnp.float32)
    active = (jax.nn.silu(gate_val) * up_val).astype(jnp.bfloat16)
    return jnp.einsum("tf,df->td", active, s_out, preferred_element_type=jnp.float32)


def combine_slots(values, places, weights, topk):
    picked = values[places].reshape(-1, topk, values.shape[1])
    return jnp.sum(picked * weights[:, :, None], axis=1)


def slotted_shards(
    attn,
    o_weight,
    residual,
    norm_gain,
    routes,
    route_logits,
    expert_in,
    expert_out,
    shared_in,
    shared_out,
):
    tok_rows = residual.shape[0]
    width = residual.shape[1]
    topk = routes.shape[1]
    tp_count = lax.axis_size("tp")
    ep_count = lax.axis_size("ep")
    local_experts = expert_in.shape[0]
    experts = local_experts * ep_count
    capacity = max(2, (4 * tok_rows * topk + 3 * experts - 1) // (3 * experts))
    attn_out = lax.psum_scatter(
        jnp.dot(attn, o_weight, preferred_element_type=jnp.float32),
        "tp",
        scatter_dimension=0,
        tiled=True,
    )
    hidden = residual.astype(jnp.float32) + attn_out
    inv_norm = lax.rsqrt(jnp.mean(hidden * hidden, axis=-1, keepdims=True) + 1e-06)
    normed = (hidden * inv_norm * norm_gain).astype(jnp.bfloat16)
    group_rows = lax.all_gather(normed, "tp", axis=0, tiled=True)
    group_cap = tp_count * capacity
    places = slot_places(routes, group_cap, experts)
    outgoing = fill_slots(group_rows, places, group_cap, experts, topk)
    incoming = lax.all_to_all(outgoing, "ep", split_axis=0, concat_axis=0, tiled=True)
    partial_value = expert_part(
        incoming.reshape(ep_count, local_experts, group_cap, width), expert_in, expert_out
    )
    returned = lax.all_to_all(
        partial_value.reshape(-1, width), "ep", split_axis=0, concat_axis=0, tiled=True
    )
    mixture = combine_slots(returned, places, route_weights(route_logits), topk)
    mixture = mixture + shared_part(group_rows, shared_in, shared_out)
    moe_sum = lax.psum_scatter(mixture, "tp", scatter_dimension=0, tiled=True)
    return (hidden + moe_sum).astype(jnp.bfloat16)


def place():
    ep = lax.axis_index("ep")
    return lax.div(ep, 4), lax.rem(lax.div(ep, 2), 2), lax.rem(ep, 2), lax.axis_index("tp")


def device_at(z, x, core, y):
    return (z * 4 + x * 2 + core, y)


def peers(z, x, core, y):
    along_z = [device_at(lax.rem(z + step, 4), x, core, y) for step in (1, 2, 3)]
    return (
        along_z,
        device_at(z, 1 - x, core, y),
        device_at(z, x, 1 - core, y),
        device_at(z, x, core, 1 - y),
    )


def greet(along_z, x_peer, core_peer, y_peer):
    barrier = pltpu.get_barrier_semaphore()
    for peer in (*along_z, x_peer, core_peer, y_peer):
        pl.semaphore_signal(
            barrier, inc=1, device_id=peer, device_id_type=pl.DeviceIdType.MESH
        )
    pl.semaphore_wait(barrier, 6)


def remote(src, dst, send_sem, recv_sem, peer):
    copy = pltpu.make_async_remote_copy(
        src_ref=src,
        dst_ref=dst,
        send_sem=send_sem,
        recv_sem=recv_sem,
        device_id=peer,
        device_id_type=pl.DeviceIdType.MESH,
    )
    copy.start()
    return copy


def gather_kernel(
    in_ref, w_ref, out_ref, w_out, own_sem, z_send, z_recv, send, recv, w_send, w_recv
):
    z, x, core, y = place()
    along_z, x_peer, core_peer, y_peer = peers(z, x, core, y)
    ep = lax.axis_index("ep")
    rows = in_ref.shape[0] // PIECES
    own = pltpu.make_async_copy(in_ref, out_ref.at[z, x, core, y], own_sem)
    own.start()
    others = [lax.rem(ep + step, 16) for step in range(1, 16)]
    barrier = pltpu.get_barrier_semaphore()
    for peer in [(other, y) for other in others] + [y_peer]:
        pl.semaphore_signal(
            barrier, inc=1, device_id=peer, device_id_type=pl.DeviceIdType.MESH
        )
    pl.semaphore_wait(barrier, 16)
    started = []
    z_copies = []
    for q in range(PIECES):
        piece = pl.ds(q * rows, rows)
        z_copies.append(
            [
                remote(
                    in_ref.at[piece],
                    out_ref.at[z, x, core, y, piece],
                    z_send.at[q, i],
                    z_recv.at[q, i],
                    along_z[i],
                )
                for i in range(3)
            ]
        )
        started.extend(z_copies[q])
    w_copies = [
        remote(w_ref.at[other], w_out.at[ep], w_send.at[i], w_recv.at[i], (other, y))
        for i, other in enumerate(others)
    ]
    w_out[ep] = w_ref[ep]
    own.wait()
    waiting = [None] * PIECES
    for turn in range(PIECES + 3):
        for stage in range(3, -1, -1):
            q = turn - stage
            if q < 0 or q >= PIECES:
                continue
            piece = pl.ds(q * rows, rows)
            if stage == 0:
                for copy in z_copies[q]:
                    copy.wait_recv()
                part = out_ref.at[:, x, core, y, piece]
                peer = x_peer if q % 2 == 0 else y_peer
            else:
                waiting[q].wait_recv()
                started.append(waiting[q])
                if stage == 1 and q % 2 == 0:
                    part, peer = out_ref.at[:, :, core, y, piece], y_peer
                elif stage == 1:
                    part, peer = out_ref.at[:, x, core, :, piece], x_peer
                else:
                    part, peer = out_ref.at[:, :, core, :, piece], core_peer
            if stage < 3:
                waiting[q] = remote(part, part, send.at[q, stage], recv.at[q, stage], peer)
    for copy in w_copies:
        copy.wait_recv()
        started.append(copy)
    for copy in started:
        copy.wait_send()


def gather_rows(normed, weights):
    rows, width = normed.shape
    out, gathered = pl.pallas_call(
        gather_kernel,
        out_shape=(
            jax.ShapeDtypeStruct((4, 2, 2, 2, rows, width), normed.dtype),
            jax.ShapeDtypeStruct(weights.shape, weights.dtype),
        ),
        in_specs=[pl.BlockSpec(memory_space=pltpu.VMEM)] * 2,
        out_specs=(
            pl.BlockSpec(memory_space=pl.ANY),
            pl.BlockSpec(memory_space=pltpu.VMEM),
        ),
        scratch_shapes=[
            pltpu.SemaphoreType.DMA,
            pltpu.SemaphoreType.DMA((PIECES, 3)),
            pltpu.SemaphoreType.DMA((PIECES, 3)),
            pltpu.SemaphoreType.DMA((PIECES, 3)),
            pltpu.SemaphoreType.DMA((PIECES, 3)),
            pltpu.SemaphoreType.DMA((15,)),
            pltpu.SemaphoreType.DMA((15,)),
        ],
        compiler_params=pltpu.CompilerParams(collective_id=0, has_side_effects=True),
    )(normed, weights)
    return out.reshape(-1, width), gathered


def scatter_kernel(
    in_ref, out_ref, in0, in1, in2, in3, sum1, sum2, sum3, z_send, z_recv, send, recv
):
    z, x, core, y = place()
    along_z, x_peer, core_peer, y_peer = peers(z, x, core, y)
    rows = in_ref.shape[4] // PIECES
    f32 = jnp.float32
    greet(along_z, x_peer, core_peer, y_peer)
    started = []
    waiting = []
    for q in range(PIECES):
        part = in_ref.at[:, :, 1 - core, :, pl.ds(q * rows, rows)]
        waiting.append(remote(part, in0.at[q], send.at[q, 0], recv.at[q, 0], core_peer))

    def after_core(q):
        piece = pl.ds(q * rows, rows)

        def add_core(i, carry):
            a, b, c = lax.div(i, 4), lax.rem(lax.div(i, 2), 2), lax.rem(i, 2)
            total = in_ref[a, b, core, c, piece].astype(f32) + in0[q, a, b, c].astype(f32)
            sum1[q, a, b, c] = total.astype(sum1.dtype)
            return carry

        lax.fori_loop(0, 16, add_core, 0)
        if q % 2 == 0:
            part, peer = sum1.at[q, :, 1 - x], x_peer
        else:
            part, peer = sum1.at[q, :, :, 1 - y], y_peer
        return remote(part, in1.at[q], send.at[q, 1], recv.at[q, 1], peer)

    def after_first(q):
        def add_first(i, carry):
            a, b = lax.div(i, 2), lax.rem(i, 2)
            mine = sum1[q, a, x, b] if q % 2 == 0 else sum1[q, a, b, y]
            sum2[q, a, b] = (mine.astype(f32) + in1[q, a, b].astype(f32)).astype(sum2.dtype)
            return carry

        lax.fori_loop(0, 8, add_first, 0)
        if q % 2 == 0:
            part, peer = sum2.at[q, :, 1 - y], y_peer
        else:
            part, peer = sum2.at[q, :, 1 - x], x_peer
        return remote(part, in2.at[q], send.at[q, 2], recv.at[q, 2], peer)

    def after_second(q):
        keep = y if q % 2 == 0 else x

        def add_second(a, carry):
            total = sum2[q, a, keep].astype(f32) + in2[q, a].astype(f32)
            sum3[q, a] = total.astype(sum3.dtype)
            return carry

        lax.fori_loop(0, 4, add_second, 0)
        return [
            remote(
                sum3.at[q, lax.rem(z + i + 1, 4)],
                in3.at[q, i],
                z_send.at[q, i],
                z_recv.at[q, i],
                along_z[i],
            )
            for i in range(3)
        ]

    def after_z(q):
        total = sum3[q, z].astype(f32) + in3[q, 0].astype(f32)
        total = total + (in3[q, 1].astype(f32) + in3[q, 2].astype(f32))
        out_ref[pl.ds(q * rows, rows)] = total

    for turn in range(PIECES + 3):
        for stage in range(4):
            q = turn - stage
            if q < 0 or q >= PIECES:
                continue
            if stage < 3:
                waiting[q].wait_recv()
                started.append(waiting[q])
                waiting[q] = (after_core, after_first, after_second)[stage](q)
            else:
                for copy in waiting[q]:
                    copy.wait_recv()
                    started.append(copy)
                after_z(q)
    for copy in started:
        copy.wait_send()


def scatter_sum(partial):
    rows, width = partial.shape[0] // 32, partial.shape[1]
    piece = (rows // PIECES, width)
    kind = partial.dtype
    return pl.pallas_call(
        scatter_kernel,
        out_shape=jax.ShapeDtypeStruct((rows, width), jnp.float32),
        in_specs=[pl.BlockSpec(memory_space=pltpu.VMEM)],
        out_specs=pl.BlockSpec(memory_space=pltpu.VMEM),
        scratch_shapes=[
            pltpu.VMEM((PIECES, 4, 2, 2, *piece), kind),
            pltpu.VMEM((PIECES, 4, 2, *piece), kind),
            pltpu.VMEM((PIECES, 4, *piece), kind),
            pltpu.VMEM((PIECES, 3, *piece), kind),
            pltpu.VMEM((PIECES, 4, 2, 2, *piece), kind),
            pltpu.VMEM((PIECES, 4, 2, *piece), kind),
            pltpu.VMEM((PIECES, 4, *piece), kind),
            pltpu.SemaphoreType.DMA((PIECES, 3)),
            pltpu.SemaphoreType.DMA((PIECES, 3)),
            pltpu.SemaphoreType.DMA((PIECES, 3)),
            pltpu.SemaphoreType.DMA((PIECES, 3)),
        ],
        compiler_params=pltpu.CompilerParams(
            collective_id=1, has_side_effects=True, vmem_limit_bytes=60 * 1024 * 1024
        ),
    )(partial.reshape(4, 2, 2, 2, rows, width))


def tp_sum_scatter(rows):
    count = lax.axis_size("tp")
    if count != 2:
        return lax.psum_scatter(rows, "tp", scatter_dimension=0, tiled=True)
    me = lax.axis_index("tp")
    each = rows.shape[0] // count
    away = lax.dynamic_slice_in_dim(rows, (1 - me) * each, each, 0).astype(jnp.bfloat16)
    arrived = lax.ppermute(away, "tp", [(0, 1), (1, 0)])
    own = lax.dynamic_slice_in_dim(rows, me * each, each, 0)
    return own + arrived.astype(jnp.float32)


def dense_shards(
    attn,
    o_weight,
    residual,
    norm_gain,
    routes,
    route_logits,
    expert_in,
    expert_out,
    shared_in,
    shared_out,
):
    local_experts = expert_in.shape[0]
    ep_count = lax.axis_size("ep")
    experts = local_experts * ep_count
    ep_me = lax.axis_index("ep")
    weights = route_weights(route_logits)
    chosen = routes[:, :, None] == jnp.arange(experts, dtype=jnp.int32)[None, None, :]
    dense_weights = jnp.sum(jnp.where(chosen, weights[:, :, None], 0.0), axis=1)
    out_weights = jnp.broadcast_to(dense_weights.T[:, None, :], (experts, 8, routes.shape[0]))

    attn_out = tp_sum_scatter(jnp.dot(attn, o_weight, preferred_element_type=jnp.float32))
    hidden = residual.astype(jnp.float32) + attn_out
    inv_norm = lax.rsqrt(jnp.mean(hidden * hidden, axis=-1, keepdims=True) + 1e-06)
    normed = (hidden * inv_norm * norm_gain).astype(jnp.bfloat16)
    all_rows, all_weights = gather_rows(normed, out_weights)
    my_weights = all_weights[:, 0, :].reshape(-1, 1)
    group = routes.shape[0]
    group_rows = lax.dynamic_slice_in_dim(all_rows, ep_me * group, group, 0)
    shared = shared_part(group_rows, shared_in, shared_out)
    partial = None
    for item in range(local_experts):
        gate_val = jnp.dot(all_rows, expert_in[item, 0], preferred_element_type=jnp.float32)
        up_val = jnp.dot(all_rows, expert_in[item, 1], preferred_element_type=jnp.float32)
        active = (jax.nn.silu(gate_val) * up_val).astype(jnp.bfloat16)
        value = jnp.einsum("tf,df->td", active, expert_out[item], preferred_element_type=jnp.float32)
        value = value * my_weights[:, item : item + 1]
        partial = value if partial is None else partial + value
    partial = partial.astype(jnp.bfloat16)
    own = lax.dynamic_slice_in_dim(partial, ep_me * group, group, 0).astype(jnp.float32) + shared
    partial = lax.dynamic_update_slice_in_dim(
        partial, own.astype(jnp.bfloat16), ep_me * group, 0
    )
    return (hidden + scatter_sum(partial)).astype(jnp.bfloat16)


def shards(*args):
    routes, expert_in = args[4], args[6]
    experts = expert_in.shape[0] * lax.axis_size("ep")
    spans = lax.axis_size("ep") == 16 and lax.axis_size("tp") == 2
    if spans and experts <= 4 * routes.shape[1]:
        return dense_shards(*args)
    return slotted_shards(*args)


def solution(mesh):
    in_specs = (
        P("ep", "tp"),
        P("tp", None),
        P(("ep", "tp"), None),
        P(),
        P("ep", None),
        P("ep", None),
        P("ep", None, None, "tp"),
        P("ep", None, "tp"),
        P(None, None, "tp"),
        P(None, "tp"),
    )
    out_specs = P(("ep", "tp"), None)
    return jax.shard_map(shards, mesh=mesh, in_specs=in_specs, out_specs=out_specs, check_vma=False)
```

```python
import jax
import jax.numpy as jnp
from jax import lax
from jax.experimental import pallas as pl
from jax.experimental.pallas import tpu as pltpu
from jax.sharding import PartitionSpec as P

PIECES = 4
GATHER_STEPS = (0, 2, 5, 8)


def slot_places(route_rows, capacity, experts):
    flat_routes = route_rows.reshape(-1)
    onehot = (flat_routes[:, None] == jnp.arange(experts, dtype=jnp.int32)[None, :]).astype(
        jnp.int32
    )
    before = jnp.cumsum(onehot, axis=0) - onehot
    ranks = jnp.sum(before * onehot, axis=1)
    return flat_routes * capacity + ranks


def fill_slots(source_rows, places, capacity, experts, topk):
    copies = jnp.repeat(source_rows, topk, axis=0)
    empty_slots = jnp.zeros((experts * capacity, source_rows.shape[1]), source_rows.dtype)
    return empty_slots.at[places].set(copies)


def route_weights(logits):
    sigmoids = jax.nn.sigmoid(logits)
    return 2.446 * sigmoids / jnp.sum(sigmoids, axis=-1, keepdims=True)


def expert_part(slots, w_in, w_out):
    gate_val = jnp.einsum("slcd,ldf->slcf", slots, w_in[:, 0], preferred_element_type=jnp.float32)
    up_val = jnp.einsum("slcd,ldf->slcf", slots, w_in[:, 1], preferred_element_type=jnp.float32)
    active = (jax.nn.silu(gate_val) * up_val).astype(jnp.bfloat16)
    return jnp.einsum("slcf,ldf->slcd", active, w_out, preferred_element_type=jnp.float32)


def shared_part(source_rows, s_in, s_out):
    gate_val = jnp.dot(source_rows, s_in[0], preferred_element_type=jnp.float32)
    up_val = jnp.dot(source_rows, s_in[1], preferred_element_type=jnp.float32)
    active = (jax.nn.silu(gate_val) * up_val).astype(jnp.bfloat16)
    return jnp.einsum("tf,df->td", active, s_out, preferred_element_type=jnp.float32)


def combine_slots(values, places, weights, topk):
    picked = values[places].reshape(-1, topk, values.shape[1])
    return jnp.sum(picked * weights[:, :, None], axis=1)


def slotted_shards(
    attn,
    o_weight,
    residual,
    norm_gain,
    routes,
    route_logits,
    expert_in,
    expert_out,
    shared_in,
    shared_out,
):
    tok_rows = residual.shape[0]
    width = residual.shape[1]
    topk = routes.shape[1]
    tp_count = lax.axis_size("tp")
    ep_count = lax.axis_size("ep")
    local_experts = expert_in.shape[0]
    experts = local_experts * ep_count
    capacity = max(2, (4 * tok_rows * topk + 3 * experts - 1) // (3 * experts))
    attn_out = lax.psum_scatter(
        jnp.dot(attn, o_weight, preferred_element_type=jnp.float32),
        "tp",
        scatter_dimension=0,
        tiled=True,
    )
    hidden = residual.astype(jnp.float32) + attn_out
    inv_norm = lax.rsqrt(jnp.mean(hidden * hidden, axis=-1, keepdims=True) + 1e-06)
    normed = (hidden * inv_norm * norm_gain).astype(jnp.bfloat16)
    group_rows = lax.all_gather(normed, "tp", axis=0, tiled=True)
    group_cap = tp_count * capacity
    places = slot_places(routes, group_cap, experts)
    outgoing = fill_slots(group_rows, places, group_cap, experts, topk)
    incoming = lax.all_to_all(outgoing, "ep", split_axis=0, concat_axis=0, tiled=True)
    partial_value = expert_part(
        incoming.reshape(ep_count, local_experts, group_cap, width), expert_in, expert_out
    )
    returned = lax.all_to_all(
        partial_value.reshape(-1, width), "ep", split_axis=0, concat_axis=0, tiled=True
    )
    mixture = combine_slots(returned, places, route_weights(route_logits), topk)
    mixture = mixture + shared_part(group_rows, shared_in, shared_out)
    moe_sum = lax.psum_scatter(mixture, "tp", scatter_dimension=0, tiled=True)
    return (hidden + moe_sum).astype(jnp.bfloat16)


def place():
    ep = lax.axis_index("ep")
    return lax.div(ep, 4), lax.rem(lax.div(ep, 2), 2), lax.rem(ep, 2), lax.axis_index("tp")


def device_at(z, x, core, y):
    return (z * 4 + x * 2 + core, y)


def peers(z, x, core, y):
    along_z = [device_at(lax.rem(z + step, 4), x, core, y) for step in (1, 2, 3)]
    return (
        along_z,
        device_at(z, 1 - x, core, y),
        device_at(z, x, 1 - core, y),
        device_at(z, x, core, 1 - y),
    )


def greet(along_z, x_peer, core_peer, y_peer):
    barrier = pltpu.get_barrier_semaphore()
    for peer in (*along_z, x_peer, core_peer, y_peer):
        pl.semaphore_signal(
            barrier, inc=1, device_id=peer, device_id_type=pl.DeviceIdType.MESH
        )
    pl.semaphore_wait(barrier, 6)


def remote(src, dst, send_sem, recv_sem, peer):
    copy = pltpu.make_async_remote_copy(
        src_ref=src,
        dst_ref=dst,
        send_sem=send_sem,
        recv_sem=recv_sem,
        device_id=peer,
        device_id_type=pl.DeviceIdType.MESH,
    )
    copy.start()
    return copy


def gather_kernel(
    in_ref, w_ref, out_ref, w_out, own_sem, z_send, z_recv, send, recv, w_send, w_recv
):
    z, x, core, y = place()
    along_z, x_peer, core_peer, y_peer = peers(z, x, core, y)
    ep = lax.axis_index("ep")
    rows = in_ref.shape[0] // PIECES
    own = pltpu.make_async_copy(in_ref, out_ref.at[z, x, core, y], own_sem)
    own.start()
    others = [lax.rem(ep + step, 16) for step in range(1, 16)]
    barrier = pltpu.get_barrier_semaphore()
    for peer in [(other, y) for other in others] + [y_peer]:
        pl.semaphore_signal(
            barrier, inc=1, device_id=peer, device_id_type=pl.DeviceIdType.MESH
        )
    pl.semaphore_wait(barrier, 16)
    started = []
    z_copies = []
    for q in range(PIECES):
        piece = pl.ds(q * rows, rows)
        z_copies.append(
            [
                remote(
                    in_ref.at[piece],
                    out_ref.at[z, x, core, y, piece],
                    z_send.at[q, i],
                    z_recv.at[q, i],
                    along_z[i],
                )
                for i in range(3)
            ]
        )
        started.extend(z_copies[q])
    w_copies = [
        remote(w_ref.at[other], w_out.at[ep], w_send.at[i], w_recv.at[i], (other, y))
        for i, other in enumerate(others)
    ]
    w_out[ep] = w_ref[ep]
    own.wait()
    waiting = [None] * PIECES
    order = sorted(
        ((stage, q) for stage in range(4) for q in range(PIECES)),
        key=lambda item: (item[1] + GATHER_STEPS[item[0]], item[0]),
    )
    for stage, q in order:
        piece = pl.ds(q * rows, rows)
        if stage == 0:
            for copy in z_copies[q]:
                copy.wait_recv()
            part = out_ref.at[:, x, core, y, piece]
            peer = x_peer if q % 2 == 0 else y_peer
        else:
            waiting[q].wait_recv()
            started.append(waiting[q])
            if stage == 1 and q % 2 == 0:
                part, peer = out_ref.at[:, :, core, y, piece], y_peer
            elif stage == 1:
                part, peer = out_ref.at[:, x, core, :, piece], x_peer
            else:
                part, peer = out_ref.at[:, :, core, :, piece], core_peer
        if stage < 3:
            waiting[q] = remote(part, part, send.at[q, stage], recv.at[q, stage], peer)
    for copy in w_copies:
        copy.wait_recv()
        started.append(copy)
    for copy in started:
        copy.wait_send()


def gather_rows(normed, weights):
    rows, width = normed.shape
    out, gathered = pl.pallas_call(
        gather_kernel,
        out_shape=(
            jax.ShapeDtypeStruct((4, 2, 2, 2, rows, width), normed.dtype),
            jax.ShapeDtypeStruct(weights.shape, weights.dtype),
        ),
        in_specs=[pl.BlockSpec(memory_space=pltpu.VMEM)] * 2,
        out_specs=(
            pl.BlockSpec(memory_space=pl.ANY),
            pl.BlockSpec(memory_space=pltpu.VMEM),
        ),
        scratch_shapes=[
            pltpu.SemaphoreType.DMA,
            pltpu.SemaphoreType.DMA((PIECES, 3)),
            pltpu.SemaphoreType.DMA((PIECES, 3)),
            pltpu.SemaphoreType.DMA((PIECES, 3)),
            pltpu.SemaphoreType.DMA((PIECES, 3)),
            pltpu.SemaphoreType.DMA((15,)),
            pltpu.SemaphoreType.DMA((15,)),
        ],
        compiler_params=pltpu.CompilerParams(collective_id=0, has_side_effects=True),
    )(normed, weights)
    return out.reshape(-1, width), gathered


def scatter_kernel(
    in_ref, out_ref, in0, in1, in2, in3, sum1, sum2, sum3, z_send, z_recv, send, recv
):
    z, x, core, y = place()
    along_z, x_peer, core_peer, y_peer = peers(z, x, core, y)
    rows = in_ref.shape[4] // PIECES
    f32 = jnp.float32
    greet(along_z, x_peer, core_peer, y_peer)
    started = []
    waiting = []
    for q in range(PIECES):
        part = in_ref.at[:, :, 1 - core, :, pl.ds(q * rows, rows)]
        waiting.append(remote(part, in0.at[q], send.at[q, 0], recv.at[q, 0], core_peer))

    def after_core(q):
        piece = pl.ds(q * rows, rows)

        def add_core(i, carry):
            a, b, c = lax.div(i, 4), lax.rem(lax.div(i, 2), 2), lax.rem(i, 2)
            total = in_ref[a, b, core, c, piece].astype(f32) + in0[q, a, b, c].astype(f32)
            sum1[q, a, b, c] = total.astype(sum1.dtype)
            return carry

        lax.fori_loop(0, 16, add_core, 0)
        if q % 2 == 0:
            part, peer = sum1.at[q, :, 1 - x], x_peer
        else:
            part, peer = sum1.at[q, :, :, 1 - y], y_peer
        return remote(part, in1.at[q], send.at[q, 1], recv.at[q, 1], peer)

    def after_first(q):
        def add_first(i, carry):
            a, b = lax.div(i, 2), lax.rem(i, 2)
            mine = sum1[q, a, x, b] if q % 2 == 0 else sum1[q, a, b, y]
            sum2[q, a, b] = (mine.astype(f32) + in1[q, a, b].astype(f32)).astype(sum2.dtype)
            return carry

        lax.fori_loop(0, 8, add_first, 0)
        if q % 2 == 0:
            part, peer = sum2.at[q, :, 1 - y], y_peer
        else:
            part, peer = sum2.at[q, :, 1 - x], x_peer
        return remote(part, in2.at[q], send.at[q, 2], recv.at[q, 2], peer)

    def after_second(q):
        keep = y if q % 2 == 0 else x

        def add_second(a, carry):
            total = sum2[q, a, keep].astype(f32) + in2[q, a].astype(f32)
            sum3[q, a] = total.astype(sum3.dtype)
            return carry

        lax.fori_loop(0, 4, add_second, 0)
        return [
            remote(
                sum3.at[q, lax.rem(z + i + 1, 4)],
                in3.at[q, i],
                z_send.at[q, i],
                z_recv.at[q, i],
                along_z[i],
            )
            for i in range(3)
        ]

    def after_z(q):
        total = sum3[q, z].astype(f32) + in3[q, 0].astype(f32)
        total = total + (in3[q, 1].astype(f32) + in3[q, 2].astype(f32))
        out_ref[pl.ds(q * rows, rows)] = total

    for turn in range(PIECES + 3):
        for stage in range(4):
            q = turn - stage
            if q < 0 or q >= PIECES:
                continue
            if stage < 3:
                waiting[q].wait_recv()
                started.append(waiting[q])
                waiting[q] = (after_core, after_first, after_second)[stage](q)
            else:
                for copy in waiting[q]:
                    copy.wait_recv()
                    started.append(copy)
                after_z(q)
    for copy in started:
        copy.wait_send()


def scatter_sum(partial):
    rows, width = partial.shape[0] // 32, partial.shape[1]
    piece = (rows // PIECES, width)
    kind = partial.dtype
    return pl.pallas_call(
        scatter_kernel,
        out_shape=jax.ShapeDtypeStruct((rows, width), jnp.float32),
        in_specs=[pl.BlockSpec(memory_space=pltpu.VMEM)],
        out_specs=pl.BlockSpec(memory_space=pltpu.VMEM),
        scratch_shapes=[
            pltpu.VMEM((PIECES, 4, 2, 2, *piece), kind),
            pltpu.VMEM((PIECES, 4, 2, *piece), kind),
            pltpu.VMEM((PIECES, 4, *piece), kind),
            pltpu.VMEM((PIECES, 3, *piece), kind),
            pltpu.VMEM((PIECES, 4, 2, 2, *piece), kind),
            pltpu.VMEM((PIECES, 4, 2, *piece), kind),
            pltpu.VMEM((PIECES, 4, *piece), kind),
            pltpu.SemaphoreType.DMA((PIECES, 3)),
            pltpu.SemaphoreType.DMA((PIECES, 3)),
            pltpu.SemaphoreType.DMA((PIECES, 3)),
            pltpu.SemaphoreType.DMA((PIECES, 3)),
        ],
        compiler_params=pltpu.CompilerParams(
            collective_id=1, has_side_effects=True, vmem_limit_bytes=60 * 1024 * 1024
        ),
    )(partial.reshape(4, 2, 2, 2, rows, width))


def tp_sum_scatter(rows):
    count = lax.axis_size("tp")
    if count != 2:
        return lax.psum_scatter(rows, "tp", scatter_dimension=0, tiled=True)
    me = lax.axis_index("tp")
    each = rows.shape[0] // count
    away = lax.dynamic_slice_in_dim(rows, (1 - me) * each, each, 0).astype(jnp.bfloat16)
    arrived = lax.ppermute(away, "tp", [(0, 1), (1, 0)])
    own = lax.dynamic_slice_in_dim(rows, me * each, each, 0)
    return own + arrived.astype(jnp.float32)


def dense_shards(
    attn,
    o_weight,
    residual,
    norm_gain,
    routes,
    route_logits,
    expert_in,
    expert_out,
    shared_in,
    shared_out,
):
    local_experts = expert_in.shape[0]
    ep_count = lax.axis_size("ep")
    experts = local_experts * ep_count
    ep_me = lax.axis_index("ep")
    weights = route_weights(route_logits)
    chosen = routes[:, :, None] == jnp.arange(experts, dtype=jnp.int32)[None, None, :]
    dense_weights = jnp.sum(jnp.where(chosen, weights[:, :, None], 0.0), axis=1)
    out_weights = jnp.broadcast_to(dense_weights.T[:, None, :], (experts, 8, routes.shape[0]))

    attn_out = tp_sum_scatter(jnp.dot(attn, o_weight, preferred_element_type=jnp.float32))
    hidden = residual.astype(jnp.float32) + attn_out
    inv_norm = lax.rsqrt(jnp.mean(hidden * hidden, axis=-1, keepdims=True) + 1e-06)
    normed = (hidden * inv_norm * norm_gain).astype(jnp.bfloat16)
    all_rows, all_weights = gather_rows(normed, out_weights)
    my_weights = all_weights[:, 0, :].reshape(-1, 1)
    group = routes.shape[0]
    group_rows = lax.dynamic_slice_in_dim(all_rows, ep_me * group, group, 0)
    shared = shared_part(group_rows, shared_in, shared_out)
    partial = None
    for item in range(local_experts):
        gate_val = jnp.dot(all_rows, expert_in[item, 0], preferred_element_type=jnp.float32)
        up_val = jnp.dot(all_rows, expert_in[item, 1], preferred_element_type=jnp.float32)
        active = (jax.nn.silu(gate_val) * up_val).astype(jnp.bfloat16)
        value = jnp.einsum("tf,df->td", active, expert_out[item], preferred_element_type=jnp.float32)
        value = value * my_weights[:, item : item + 1]
        partial = value if partial is None else partial + value
    partial = partial.astype(jnp.bfloat16)
    own = lax.dynamic_slice_in_dim(partial, ep_me * group, group, 0).astype(jnp.float32) + shared
    partial = lax.dynamic_update_slice_in_dim(
        partial, own.astype(jnp.bfloat16), ep_me * group, 0
    )
    return (hidden + scatter_sum(partial)).astype(jnp.bfloat16)


def shards(*args):
    routes, expert_in = args[4], args[6]
    experts = expert_in.shape[0] * lax.axis_size("ep")
    spans = lax.axis_size("ep") == 16 and lax.axis_size("tp") == 2
    if spans and experts <= 4 * routes.shape[1]:
        return dense_shards(*args)
    return slotted_shards(*args)


def solution(mesh):
    in_specs = (
        P("ep", "tp"),
        P("tp", None),
        P(("ep", "tp"), None),
        P(),
        P("ep", None),
        P("ep", None),
        P("ep", None, None, "tp"),
        P("ep", None, "tp"),
        P(None, None, "tp"),
        P(None, "tp"),
    )
    out_specs = P(("ep", "tp"), None)
    return jax.shard_map(shards, mesh=mesh, in_specs=in_specs, out_specs=out_specs, check_vma=False)
```
